32 devices in a mesh: grp: 2 (over core), seq: 8 (over z, y), tp: 2 (over x).
Axes of the slice: x: 2, y: 2, z: 4, core: 2. Of those that a mesh axis runs over, the one named last changes fastest.
Arguments:
- prompt_states: bfloat16 [2, 16384, 4096], P(None, ('grp', 'seq'), 'tp'), may hold values from -40 to 40
- q_weight: bfloat16 [4096, 16, 128], P(None, 'tp'), may hold values from -0.09375 to 0.09375
- kv_weight: bfloat16 [4096, 2, 4, 128], P(None, None, 'tp'), may hold values from -0.09375 to 0.09375
- lengths: int32 [2], replicated, may hold values from 4096 to 16384, as said below
- sink_positions: int32 [2, 4], replicated, may hold values from 0 to 2047
Outputs:
- attended: bfloat16 [2, 16384, 2048], P(None, ('grp', 'seq'), 'tp')
- kv_cache: bfloat16 [2, 4, 2, 8, 1024, 256], P(None, ('tp', 'grp'), None, 'seq')
The draws below stay inside these ranges and needn't reach their ends.
Inputs may be any that keep to these rules, and one draw needn't show every extreme that they name: `lengths`: at least one request has length 16384.
All inputs are finite; a program needn't handle non-finite values.
Results may differ from the reference program's by a relative error of at most 0.0065.
Values may be sent and summed in bfloat16 or wider, within the bound.
No kernel may reach another device: no remote copies, remote signals or barrier semaphores. Data moves between devices by JAX's collectives and lax.ppermute only.
A program may use at most 512 MiB of HBM per device.

```python
import math
import jax
import jax.numpy as jnp
from jax import lax

D = 4096
HD = 128
QH = 16
KVH = 4
SINKS = 4
WINDOW = 4096
REQS = 2
LEN = 16384
SLAB = 1024
N_GRP = 2
N_SEQ = 8


def draw_prompt_states(key, part):
    scale_key, base_key = jax.random.split(jax.random.fold_in(key, 17), 2)
    scales = jnp.exp(jax.random.uniform(scale_key, (REQS, LEN, 1), jnp.float32, 0.0, math.log(1.1)))
    states = jax.random.normal(base_key, (REQS, LEN, D), jnp.float32) * scales
    return jnp.clip(states, -40.0, 40.0).astype(jnp.bfloat16)


def draw_lengths(key, part):
    length_key, pick_key = jax.random.split(jax.random.fold_in(key, 29), 2)
    drawn = jax.random.randint(length_key, (REQS,), LEN // 4, LEN + 1, jnp.int32)
    chosen = jax.random.randint(pick_key, (), 0, REQS, jnp.int32)
    full_len = jnp.full((REQS,), LEN, jnp.int32)
    return jnp.where(jnp.arange(REQS, dtype=jnp.int32) == chosen, full_len, drawn)


def touch_ends(values, stream_key, smallest, largest):
    spot = [jax.random.randint(jax.random.fold_in(stream_key, axis), (), 0, length) for axis, length in enumerate(values.shape)]
    main_axis = values.shape.index(max(values.shape))
    beside = spot[:main_axis] + [(spot[main_axis] + 1) % values.shape[main_axis]] + spot[main_axis + 1:]
    return values.at[tuple(spot)].set(smallest).at[tuple(beside)].set(largest)


def block_levels(key, shape, cuts, low, top_value):
    def one(axis_at, blocks):
        heights = jax.random.uniform(jax.random.fold_in(jax.random.fold_in(key, 6), axis_at), (blocks,), jnp.float32, low / len(cuts), top_value / len(cuts))
        return jnp.repeat(jnp.exp(heights), shape[axis_at] // blocks).reshape((-1,) + (1,) * (len(shape) - axis_at - 1))

    level = one(*cuts[0])
    for cut in cuts[1:]:
        level = level * one(*cut)
    return level


def bell_draw(key, extent, width, most, shards=(), kind=jnp.bfloat16):
    loudness = block_levels(key, extent, shards, -0.22, 0.18) if shards else 1.0
    entries = jax.random.normal(key, extent, jnp.float32) * width * loudness
    return jnp.minimum(jnp.maximum(entries, -most), most).astype(kind)


def setup_inputs(seed: int = 0) -> dict:
    keys = jax.random.split(jax.random.key(seed), 6)
    prompt_states = draw_prompt_states(jax.random.fold_in(keys[5], 71), 0)
    q_weight = bell_draw(keys[1], (D, QH, HD), D ** -0.5, 0.09375, ((1, 2),))
    kv_weight = bell_draw(keys[2], (D, 2, KVH, HD), D ** -0.5, 0.09375, ((2, 2),))
    lengths = draw_lengths(jax.random.fold_in(keys[5], 71), 0)
    sink_positions = touch_ends(jax.random.randint(keys[4], (REQS, SINKS), 0, LEN // 8), jax.random.fold_in(keys[4], 1), 0, (LEN // 8) - 1).astype(jnp.int32)
    return dict(prompt_states=prompt_states, q_weight=q_weight, kv_weight=kv_weight, lengths=lengths, sink_positions=sink_positions)


ROPE_BASE = 10000.0
NEG_FILL = -1e+30

def rotate(vectors, positions):
    head_dim = vectors.shape[-1]
    half_dim = head_dim // 2
    ladder = jnp.arange(half_dim, dtype=jnp.float32) * (2.0 / head_dim)
    inv_freq = jnp.exp(-math.log(ROPE_BASE) * ladder)
    angles = positions.astype(jnp.float32)[:, None] * inv_freq[None, :]
    cosine = jnp.cos(angles)[None, :, None, :]
    sine_part = jnp.sin(angles)[None, :, None, :]
    lead_half = vectors[..., :half_dim]
    tail_half = vectors[..., half_dim:]
    return jnp.concatenate([lead_half * cosine - tail_half * sine_part, tail_half * cosine + lead_half * sine_part], axis=-1)

def reference(prompt_states, q_weight, kv_weight, lengths, sink_positions):
    num_reqs, length, model_width = prompt_states.shape
    num_heads, head_dim = (q_weight.shape[1], q_weight.shape[2])
    kv_heads = kv_weight.shape[2]
    share_count = num_heads // kv_heads
    flattened = prompt_states.reshape(num_reqs * length, model_width)
    query_raw = jnp.dot(flattened, q_weight.reshape(model_width, num_heads * head_dim), preferred_element_type=jnp.float32)
    kv_raw = jnp.dot(flattened, kv_weight.reshape(model_width, 2 * kv_heads * head_dim), preferred_element_type=jnp.float32)
    positions = jnp.arange(length, dtype=jnp.int32)
    queries = rotate(query_raw.reshape(num_reqs, length, num_heads, head_dim), positions).astype(jnp.bfloat16)
    kv_raw = kv_raw.reshape(num_reqs, length, 2, kv_heads, head_dim)
    key_rows = rotate(kv_raw[:, :, 0], positions).astype(jnp.bfloat16)
    values = kv_raw[:, :, 1].astype(jnp.bfloat16)
    inv_root = 1.0 / math.sqrt(head_dim)
    block_rows = 512 if length % 512 == 0 else length

    def one_request(packed):
        req_query, req_keys, req_values, prompt_len, sink_pos = packed
        sink_flag = jnp.any(positions[:, None] == sink_pos[None, :], axis=1)
        keys_wide = req_keys.astype(jnp.float32)
        values_wide = req_values.astype(jnp.float32)

        def one_block(block_index):
            start = block_index * block_rows
            query_pos = start + jnp.arange(block_rows, dtype=jnp.int32)
            block_query = lax.dynamic_slice_in_dim(req_query, start, block_rows, 0)
            distance = query_pos[:, None] - positions[None, :]
            visible = (distance >= 0) & (positions[None, :] < prompt_len) & ((distance < WINDOW) | sink_flag[None, :])
            query_wide = block_query.astype(jnp.float32).reshape(block_rows, kv_heads, share_count, head_dim)
            scores = jnp.einsum('qhgd,khd->hgqk', query_wide, keys_wide, precision=lax.Precision.HIGHEST) * inv_root
            scores = jnp.where(visible[None, None], scores, NEG_FILL)
            row_max = lax.optimization_barrier(jnp.max(scores, axis=-1, keepdims=True))
            weights = jnp.where(visible[None, None], jnp.exp(scores - row_max), 0.0)
            sums_now = lax.optimization_barrier(jnp.sum(weights, axis=-1))
            weight_rows = lax.optimization_barrier(weights.astype(jnp.bfloat16)).astype(jnp.float32)
            mixed = jnp.einsum('hgqk,khd->hgqd', weight_rows, values_wide, precision=lax.Precision.HIGHEST)
            mixed = mixed / sums_now[..., None]
            mixed = jnp.transpose(mixed, (2, 0, 1, 3)).reshape(block_rows, num_heads * head_dim)
            live_rows = query_pos < prompt_len
            return jnp.where(live_rows[:, None], mixed, 0.0).astype(jnp.bfloat16)
        blocks = lax.map(one_block, jnp.arange(length // block_rows, dtype=jnp.int32))
        return blocks.reshape(length, num_heads * head_dim)
    attended = lax.map(one_request, (queries, key_rows, values, lengths, sink_positions))
    live_rows = positions[None, :] < lengths[:, None]
    kv_cache = jnp.concatenate([key_rows, values], axis=-1)
    kv_cache = jnp.where(live_rows[:, :, None, None], kv_cache, jnp.zeros_like(kv_cache))
    kv_cache = jnp.transpose(kv_cache, (0, 2, 1, 3))
    kv_cache = kv_cache.reshape(num_reqs, kv_heads, N_GRP, N_SEQ, SLAB, 2 * head_dim)
    return (attended, kv_cache)
```

```python
import functools
import math

import jax
import jax.numpy as jnp
from jax import lax
from jax.experimental import pallas as pl
from jax.experimental.pallas import tpu as pltpu
from jax.sharding import PartitionSpec as P


WINDOW = 4096
ROPE_BASE = 10000.0
NEG_FILL = -1e30
FAR_AWAY = 1 << 30
SINK_PAD = 128
LINE = ("grp", "seq")


def rope_tables(positions, head_dim):
    half_dim = head_dim // 2
    ladder = jnp.arange(half_dim, dtype=jnp.float32) * (2.0 / head_dim)
    inv_freq = jnp.exp(-math.log(ROPE_BASE) * ladder)
    angles = positions.astype(jnp.float32)[:, None] * inv_freq[None, :]
    cosine = jnp.cos(angles)
    sine = jnp.sin(angles)
    return (
        jnp.concatenate([cosine, cosine], axis=1),
        jnp.concatenate([-sine, sine], axis=1),
    )


def turn(v, cosine, sine):
    return v * cosine + pltpu.roll(v, v.shape[-1] // 2, 1) * sine


def finish_kv_body(own_ref, other_ref, cos_ref, sin_ref, out_ref):
    head_dim = cos_ref.shape[1]
    total = own_ref[...] + other_ref[...].astype(jnp.float32)
    keys = turn(total[:, :head_dim], cos_ref[...], sin_ref[...])
    out_ref[0, :, :head_dim] = keys.astype(jnp.bfloat16)
    out_ref[0, :, head_dim:] = total[:, head_dim:].astype(jnp.bfloat16)


def finish_kv(own, other, cosine, sine, first, kv_local):
    slab, _ = own.shape
    head_dim = cosine.shape[1]
    rows = min(512, slab)
    part = pl.BlockSpec((rows, 2 * head_dim), lambda g, i: (i, first + g))
    table = pl.BlockSpec((rows, head_dim), lambda g, i: (i, 0))
    return pl.pallas_call(
        finish_kv_body,
        grid=(kv_local, slab // rows),
        in_specs=[part, part, table, table],
        out_specs=pl.BlockSpec((1, rows, 2 * head_dim), lambda g, i: (g, i, 0)),
        out_shape=jax.ShapeDtypeStruct((kv_local, slab, 2 * head_dim), jnp.bfloat16),
        cost_estimate=pl.CostEstimate(
            flops=12 * kv_local * slab * head_dim, bytes_accessed=20 * kv_local * slab * head_dim, transcendentals=0
        ),
        name="finish_kv",
    )(own, other, cosine, sine)


def attend_body(meta, own_ref, other_ref, cos_ref, sin_ref, sink_ref, sink_pos_ref, *rest,
                share, tile, slab, span, picks, n_slabs):
    slab_refs = rest[:n_slabs]
    out_ref, key_buf, val_buf, q_buf = rest[-4:]
    hd = cos_ref.shape[1]
    index, length = meta[0], meta[1]
    rows = share * tile
    window = span * slab
    scale = math.log2(math.e) / math.sqrt(hd)
    block = pl.program_id(0)
    odd = lax.rem(index, 2)

    @pl.when(block == 0)
    def _():
        def place(slot, ref):
            key_buf[slot * slab:(slot + 1) * slab, :] = ref[0, :, :hd]
            val_buf[slot * slab:(slot + 1) * slab, :hd] = ref[0, :, hd:]

        for slot, (even_pick, odd_pick) in enumerate(picks):
            if even_pick == odd_pick:
                place(slot, slab_refs[even_pick])
            else:
                pl.when(odd == 0)(functools.partial(place, slot, slab_refs[even_pick]))
                pl.when(odd == 1)(functools.partial(place, slot, slab_refs[odd_pick]))
        val_buf[:, hd:] = jnp.ones((val_buf.shape[0], hd), jnp.bfloat16)

        for slot in range(span):
            @pl.when(slot < span - index)
            def _():
                start = pl.multiple_of((span - index) * slab, slab)
                key = key_buf[pl.ds(start, 16), :][:1]
                key_buf[slot * slab:(slot + 1) * slab, :] = jnp.broadcast_to(key, (slab, hd))
                val_buf[slot * slab:(slot + 1) * slab, :] = jnp.zeros((slab, 2 * hd), jnp.bfloat16)

    parts = []
    for h in range(share):
        cols = slice(h * hd, (h + 1) * hd)
        raw = own_ref[:, cols] + other_ref[:, cols].astype(jnp.float32)
        parts.append(turn(raw, cos_ref[...], sin_ref[...]).astype(jnp.bfloat16))
    q_buf[...] = jnp.concatenate(parts, axis=0)
    base = pl.multiple_of(block * tile, tile)

    def scores(start):
        keys = key_buf[pl.ds(pl.multiple_of(start, tile), tile), :]
        return lax.dot_general(
            q_buf[...], keys, (((1,), (1,)), ((), ())), preferred_element_type=jnp.float32
        )

    def vals(start):
        return val_buf[pl.ds(pl.multiple_of(start, tile), tile), :]

    def mix(p, v):
        return jnp.dot(p.astype(jnp.bfloat16), v, preferred_element_type=jnp.float32)

    q_row = lax.broadcasted_iota(jnp.int32, (share, tile, tile), 1).reshape(rows, tile)
    k_col = lax.broadcasted_iota(jnp.int32, (rows, tile), 1)
    s_own = jnp.where(k_col <= q_row, scores(base + window), NEG_FILL)
    s_far = jnp.where(k_col > q_row, scores(base), NEG_FILL)
    s_sink = lax.dot_general(
        q_buf[...], sink_ref[0, :, :hd], (((1,), (1,)), ((), ())),
        preferred_element_type=jnp.float32,
    )
    q_pos = index * slab + base + lax.broadcasted_iota(
        jnp.int32, (share, tile, SINK_PAD), 1
    ).reshape(rows, SINK_PAD)
    s_sink = jnp.where(q_pos - sink_pos_ref[0:1, :] >= WINDOW, s_sink, NEG_FILL)
    s = jnp.concatenate([s_own, s_far, s_sink], axis=1)
    v_sink = jnp.concatenate(
        [sink_ref[0, :, hd:], jnp.ones((SINK_PAD, hd), jnp.bfloat16)], axis=1
    )
    v = jnp.concatenate([vals(base + window), vals(base), v_sink], axis=0)
    top = jnp.max(s, axis=1, keepdims=True)
    acc = mix(jnp.exp2(s * scale - top * scale), v)

    for n in range(1, window // tile):
        start = base + n * tile
        s = scores(start)
        new_top = jnp.maximum(top, jnp.max(s, axis=1, keepdims=True))
        p = jnp.exp2(s * scale - new_top * scale)
        acc = acc * jnp.exp2((top - new_top) * scale) + mix(p, vals(start))
        top = new_top

    pos = index * slab + base + lax.broadcasted_iota(jnp.int32, (tile, hd), 0)
    live = pos < length
    for h in range(share):
        piece = acc[h * tile:(h + 1) * tile]
        mixed = piece[:, :hd] / piece[:, hd:]
        out_ref[0, :, h * hd:(h + 1) * hd] = jnp.where(live, mixed, 0.0).astype(out_ref.dtype)


def attend(meta, own, other, cosine, sine, sink, sink_pos, slabs, picks, span, earlier,
           request, head, slot, num_reqs, kv_local, tile):
    slab, width = own.shape
    head_dim = cosine.shape[1]
    group = width // kv_local
    share = group // head_dim
    table = pl.BlockSpec((tile, head_dim), lambda i, m: (i, 0))
    in_specs = [
        pl.BlockSpec((tile, group), lambda i, m: (i, head)),
        pl.BlockSpec((tile, group), lambda i, m: (i, 0)),
        table,
        table,
        pl.BlockSpec((1, SINK_PAD, 2 * head_dim), lambda i, m: (head, 0, 0)),
        pl.BlockSpec((8, SINK_PAD), lambda i, m: (0, 0)),
    ] + [pl.BlockSpec((1, slab, 2 * head_dim), lambda i, m: (slot, 0, 0)) for _ in slabs]
    args = [meta, own, other, cosine, sine, sink, sink_pos, *slabs]
    aliases = {}
    if earlier is not None:
        in_specs.append(pl.BlockSpec(memory_space=pl.ANY))
        aliases = {len(args): 0}
        args.append(earlier)
    rows = share * tile
    work = (slab // tile) * rows * (span * slab + tile)
    return pl.pallas_call(
        functools.partial(
            attend_body, share=share, tile=tile, slab=slab, span=span, picks=picks,
            n_slabs=len(slabs),
        ),
        grid_spec=pltpu.PrefetchScalarGridSpec(
            num_scalar_prefetch=1,
            grid=(slab // tile,),
            in_specs=in_specs,
            out_specs=pl.BlockSpec((1, tile, group), lambda i, m: (request, i, head)),
            scratch_shapes=[
                pltpu.VMEM(((span + 1) * slab, head_dim), jnp.bfloat16),
                pltpu.VMEM(((span + 1) * slab, 2 * head_dim), jnp.bfloat16),
                pltpu.VMEM((rows, head_dim), jnp.bfloat16),
            ],
        ),
        out_shape=jax.ShapeDtypeStruct((num_reqs, slab, width), jnp.bfloat16),
        input_output_aliases=aliases,
        compiler_params=pltpu.CompilerParams(vmem_limit_bytes=48 << 20),
        cost_estimate=pl.CostEstimate(
            flops=8 * work * head_dim, bytes_accessed=8 << 20, transcendentals=work
        ),
        name="attend",
    )(*args)


def per_device(prompt_states, q_weight, kv_weight, lengths, sink_positions):
    num_reqs, slab, half = prompt_states.shape
    _, heads, hd = q_weight.shape
    kv_local = kv_weight.shape[2]
    count = lax.axis_size(LINE)
    n_grp = lax.axis_size("grp")
    n_seq = lax.axis_size("seq")
    grp, seq, tp = lax.axis_index("grp"), lax.axis_index("seq"), lax.axis_index("tp")
    index = grp * n_seq + seq
    span = (WINDOW - 1) // slab + 1
    tile = min(256, slab)
    assert n_grp == 2 and n_seq % 2 == 0 and span % 2 == 0 and lax.axis_size("tp") == 2

    def swap(x, axis):
        return lax.ppermute(x, axis, [(0, 1), (1, 0)])

    def forward(x, distance):
        return lax.ppermute(x, LINE, [(i - distance, i) for i in range(distance, count)])

    def pairs(x):
        return lax.ppermute(x, LINE, [(i, i ^ 1) for i in range(count)])

    def even_to_odd(x):
        return lax.ppermute(x, LINE, [(i, i + 1) for i in range(0, count, 2)])

    def odd_to_even(x):
        return lax.ppermute(x, LINE, [(i + 1, i) for i in range(0, count, 2)])

    def after(x, *first):
        return lax.optimization_barrier((x, *first))[0]

    def ordered(mine, theirs, place):
        return jnp.where(
            place == 0,
            jnp.concatenate([mine, theirs], axis=0),
            jnp.concatenate([theirs, mine], axis=0),
        )

    own_row, far_row = tp * half, (1 - tp) * half
    kv_piece = half // 2
    kv_sent = lax.dynamic_slice_in_dim(kv_weight, far_row + grp * kv_piece, kv_piece, 0)
    kv_got = swap(kv_sent, "tp")
    q_piece = half // 4
    side = lax.rem(seq, 2)
    q_sent = lax.dynamic_slice_in_dim(
        q_weight, far_row + (grp * 2 + side) * q_piece, q_piece, 0
    )
    q_got = swap(q_sent, "tp")

    def kv_matrix(w):
        return jnp.transpose(w, (0, 2, 1, 3)).reshape(w.shape[0], 2 * kv_local * hd)

    def q_matrix(w):
        return w.reshape(w.shape[0], heads * hd)

    def product(x, w):
        return jnp.dot(x, w, preferred_element_type=jnp.float32)

    kv_near = kv_matrix(lax.dynamic_slice_in_dim(kv_weight, own_row, half, 0))
    q_near = q_matrix(lax.dynamic_slice_in_dim(q_weight, own_row, half, 0))
    kv_own = [product(prompt_states[r], kv_near) for r in range(num_reqs)]

    positions = index * slab + jnp.arange(slab, dtype=jnp.int32)
    cosine, sine = rope_tables(positions, hd)
    mark_count = sink_positions.shape[1]
    marks = jnp.arange(mark_count)
    repeated = jnp.any(
        (sink_positions[:, :, None] == sink_positions[:, None, :])
        & (marks[None, :] < marks[:, None])[None],
        axis=2,
    )
    usable = jnp.where(repeated, FAR_AWAY, sink_positions)
    hits = (sink_positions[:, :, None] == positions[None, None, :]).astype(jnp.bfloat16)
    hits = jnp.pad(hits, ((0, 0), (0, 8 - mark_count), (0, 0)))
    sink_states = jnp.stack([
        product(hits[r], prompt_states[r]).astype(jnp.bfloat16) for r in range(num_reqs)
    ]).reshape(num_reqs * 8, half)
    distance = 1
    while distance < count:
        sink_states = sink_states + forward(sink_states, distance)
        distance *= 2
    sink_states = jnp.pad(sink_states, ((0, SINK_PAD - num_reqs * 8), (0, 0)))
    sink_slots = jnp.pad(sink_positions, ((0, 0), (0, 8 - mark_count))).reshape(-1)
    sink_slots = jnp.pad(sink_slots, (0, SINK_PAD - num_reqs * 8))
    sink_cos, sink_sin = rope_tables(sink_slots, hd)
    sink_lines = [
        jnp.broadcast_to(
            jnp.pad(
                usable[r], (r * 8, SINK_PAD - r * 8 - mark_count), constant_values=FAR_AWAY
            )[None, :],
            (8, SINK_PAD),
        )
        for r in range(num_reqs)
    ]

    kv_far = kv_matrix(ordered(kv_got, swap(kv_got, "grp"), grp))
    kv_part = [product(prompt_states[r], kv_far).astype(jnp.bfloat16) for r in range(num_reqs)]
    kv_other = [swap(kv_part[r], "tp") for r in range(num_reqs)]
    sink_own = product(sink_states, kv_near)
    sink_other = swap(product(sink_states, kv_far).astype(jnp.bfloat16), "tp")
    sinks = finish_kv(sink_own, sink_other, sink_cos, sink_sin, 0, kv_local)

    states_later = after(prompt_states, *kv_part)
    q_own = [product(states_later[r], q_near) for r in range(num_reqs)]
    q_pair = ordered(q_got, pairs(q_got), side)
    q_far = q_matrix(ordered(q_pair, swap(q_pair, "grp"), grp))
    group = heads // kv_local * hd
    q_other = [
        [
            swap(
                product(states_later[r], q_far[:, h * group:(h + 1) * group]).astype(
                    jnp.bfloat16
                ),
                "tp",
            )
            for h in range(kv_local)
        ]
        for r in range(num_reqs)
    ]

    steps = span // 2
    picks = [None] * (span + 1)

    def exchange(own):
        slabs = [own]
        relayed = [0]
        for _ in range(steps):
            slabs.append(forward(slabs[relayed[-1]], 2))
            relayed.append(len(slabs) - 1)
        slabs.append(even_to_odd(own))
        swapped = [len(slabs) - 1]
        for k in range(1, steps):
            slabs.append(pairs(slabs[relayed[k]]))
            swapped.append(len(slabs) - 1)
        slabs.append(odd_to_even(slabs[relayed[steps]]))
        last_even = len(slabs) - 1
        for k in range(steps + 1):
            picks[span - 2 * k] = (relayed[k], relayed[k])
        for k in range(1, steps + 1):
            even_pick = swapped[k] if k < steps else last_even
            picks[span - (2 * k - 1)] = (even_pick, swapped[k - 1])
        return slabs

    attended = None
    kv = []
    for r in range(num_reqs):
        meta = jnp.stack([index, lengths[r]])
        units = [(h, 1) for h in range(kv_local)] if r == 0 else [(0, kv_local)]
        mine = []
        for first, size in units:
            rows = finish_kv(kv_own[r], kv_other[r], cosine, sine, first, size)
            mine.append(rows)
            slabs = exchange(rows)
            for h in range(size):
                attended = attend(
                    meta, q_own[r], q_other[r][first + h], cosine, sine, sinks,
                    sink_lines[r], slabs, picks, span, attended, r, first + h, h,
                    num_reqs, kv_local, tile,
                )
        kv.append([m[h] for m in mine for h in range(m.shape[0])])

    lower = grp == 0
    home = jnp.stack([jnp.where(lower, kv[r][0], kv[r][1]) for r in range(num_reqs)])
    away = jnp.stack([jnp.where(lower, kv[r][1], kv[r][0]) for r in range(num_reqs)])
    came = swap(away, "grp")
    pages = jnp.stack([jnp.where(lower, home, came), jnp.where(lower, came, home)], axis=1)
    page_pos = (jnp.arange(n_grp) * n_seq + seq)[:, None] * slab + jnp.arange(slab)[None, :]
    live = page_pos[None] < lengths[:, None, None]
    pages = jnp.where(live[..., None], pages, jnp.zeros_like(pages))
    kv_cache = pages[:, None, :, None]
    return attended, kv_cache


def solution(mesh):
    placed = (
        P(None, ("grp", "seq"), "tp"),
        P(None, "tp", None),
        P(None, None, "tp", None),
        P(),
        P(),
    )

    return jax.shard_map(
        per_device,
        mesh=mesh,
        in_specs=placed,
        out_specs=(P(None, ("grp", "seq"), "tp"), P(None, ("tp", "grp"), None, "seq", None, None)),
        check_vma=False,
    )
```

```python
import functools
import math

import jax
import jax.numpy as jnp
from jax import lax
from jax.experimental import pallas as pl
from jax.experimental.pallas import tpu as pltpu
from jax.sharding import PartitionSpec as P


WINDOW = 4096
ROPE_BASE = 10000.0
NEG_FILL = -1e30
FAR_AWAY = 1 << 30
SINK_PAD = 128
LINE = ("grp", "seq")


def rope_tables(positions, head_dim):
    half_dim = head_dim // 2
    ladder = jnp.arange(half_dim, dtype=jnp.float32) * (2.0 / head_dim)
    inv_freq = jnp.exp(-math.log(ROPE_BASE) * ladder)
    angles = positions.astype(jnp.float32)[:, None] * inv_freq[None, :]
    cosine = jnp.cos(angles)
    sine = jnp.sin(angles)
    return (
        jnp.concatenate([cosine, cosine], axis=1),
        jnp.concatenate([-sine, sine], axis=1),
    )


def turn(v, cosine, sine):
    return v * cosine + pltpu.roll(v, v.shape[-1] // 2, 1) * sine


def finish_kv_body(own_ref, other_ref, cos_ref, sin_ref, out_ref):
    head_dim = cos_ref.shape[1]
    total = own_ref[...] + other_ref[...].astype(jnp.float32)
    keys = turn(total[:, :head_dim], cos_ref[...], sin_ref[...])
    out_ref[0, :, :head_dim] = keys.astype(jnp.bfloat16)
    out_ref[0, :, head_dim:] = total[:, head_dim:].astype(jnp.bfloat16)


def finish_kv(own, other, cosine, sine, first, kv_local):
    slab, _ = own.shape
    head_dim = cosine.shape[1]
    rows = min(512, slab)
    part = pl.BlockSpec((rows, 2 * head_dim), lambda g, i: (i, first + g))
    table = pl.BlockSpec((rows, head_dim), lambda g, i: (i, 0))
    return pl.pallas_call(
        finish_kv_body,
        grid=(kv_local, slab // rows),
        in_specs=[part, part, table, table],
        out_specs=pl.BlockSpec((1, rows, 2 * head_dim), lambda g, i: (g, i, 0)),
        out_shape=jax.ShapeDtypeStruct((kv_local, slab, 2 * head_dim), jnp.bfloat16),
        cost_estimate=pl.CostEstimate(
            flops=12 * kv_local * slab * head_dim, bytes_accessed=20 * kv_local * slab * head_dim, transcendentals=0
        ),
        name="finish_kv",
    )(own, other, cosine, sine)


def attend_body(meta, own_ref, other_ref, cos_ref, sin_ref, sink_ref, sink_pos_ref, *rest,
                share, tile, slab, span, picks, n_slabs):
    slab_refs = rest[:n_slabs]
    out_ref, key_buf, val_buf, q_buf = rest[-4:]
    hd = cos_ref.shape[1]
    index, length = meta[0], meta[1]
    rows = share * tile
    window = span * slab
    scale = math.log2(math.e) / math.sqrt(hd)
    block = pl.program_id(0)
    odd = lax.rem(index, 2)

    @pl.when(block == 0)
    def _():
        def place(slot, ref):
            key_buf[slot * slab:(slot + 1) * slab, :] = ref[0, :, :hd]
            val_buf[slot * slab:(slot + 1) * slab, :hd] = ref[0, :, hd:]

        for slot, (even_pick, odd_pick) in enumerate(picks):
            if even_pick == odd_pick:
                place(slot, slab_refs[even_pick])
            else:
                pl.when(odd == 0)(functools.partial(place, slot, slab_refs[even_pick]))
                pl.when(odd == 1)(functools.partial(place, slot, slab_refs[odd_pick]))
        val_buf[:, hd:] = jnp.ones((val_buf.shape[0], hd), jnp.bfloat16)

        for slot in range(span):
            @pl.when(slot < span - index)
            def _():
                start = pl.multiple_of((span - index) * slab, slab)
                key = key_buf[pl.ds(start, 16), :][:1]
                key_buf[slot * slab:(slot + 1) * slab, :] = jnp.broadcast_to(key, (slab, hd))
                val_buf[slot * slab:(slot + 1) * slab, :] = jnp.zeros((slab, 2 * hd), jnp.bfloat16)

    parts = []
    for h in range(share):
        cols = slice(h * hd, (h + 1) * hd)
        raw = own_ref[:, cols] + other_ref[:, cols].astype(jnp.float32)
        parts.append(turn(raw, cos_ref[...], sin_ref[...]).astype(jnp.bfloat16))
    q_buf[...] = jnp.concatenate(parts, axis=0)
    base = pl.multiple_of(block * tile, tile)

    def scores(start):
        keys = key_buf[pl.ds(pl.multiple_of(start, tile), tile), :]
        return lax.dot_general(
            q_buf[...], keys, (((1,), (1,)), ((), ())), preferred_element_type=jnp.float32
        )

    def vals(start):
        return val_buf[pl.ds(pl.multiple_of(start, tile), tile), :]

    def mix(p, v):
        return jnp.dot(p.astype(jnp.bfloat16), v, preferred_element_type=jnp.float32)

    q_row = lax.broadcasted_iota(jnp.int32, (share, tile, tile), 1).reshape(rows, tile)
    k_col = lax.broadcasted_iota(jnp.int32, (rows, tile), 1)
    s_own = jnp.where(k_col <= q_row, scores(base + window), NEG_FILL)
    s_far = jnp.where(k_col > q_row, scores(base), NEG_FILL)
    s_sink = lax.dot_general(
        q_buf[...], sink_ref[0, :, :hd], (((1,), (1,)), ((), ())),
        preferred_element_type=jnp.float32,
    )
    q_pos = index * slab + base + lax.broadcasted_iota(
        jnp.int32, (share, tile, SINK_PAD), 1
    ).reshape(rows, SINK_PAD)
    s_sink = jnp.where(q_pos - sink_pos_ref[0:1, :] >= WINDOW, s_sink, NEG_FILL)
    v_sink = jnp.concatenate(
        [sink_ref[0, :, hd:], jnp.ones((SINK_PAD, hd), jnp.bfloat16)], axis=1
    )

    def fold(top, acc, s, v):
        new_top = jnp.maximum(top, jnp.max(s, axis=1, keepdims=True))
        p = jnp.exp2(s * scale - new_top * scale)
        return new_top, acc * jnp.exp2((top - new_top) * scale) + mix(p, v)

    s = jnp.concatenate([s_own, s_far], axis=1)
    v = jnp.concatenate([vals(base + window), vals(base)], axis=0)
    top = jnp.max(s, axis=1, keepdims=True)
    acc = mix(jnp.exp2(s * scale - top * scale), v)
    for n in range(1, window // tile):
        start = base + n * tile
        top, acc = fold(top, acc, scores(start), vals(start))
    top, acc = fold(top, acc, s_sink, v_sink)

    pos = index * slab + base + lax.broadcasted_iota(jnp.int32, (tile, hd), 0)
    live = pos < length
    for h in range(share):
        piece = acc[h * tile:(h + 1) * tile]
        mixed = piece[:, :hd] / piece[:, hd:]
        out_ref[0, :, h * hd:(h + 1) * hd] = jnp.where(live, mixed, 0.0).astype(out_ref.dtype)


def attend(meta, own, other, cosine, sine, sink, sink_pos, slabs, picks, span, earlier,
           request, head, slot, num_reqs, kv_local, tile):
    slab, width = own.shape
    head_dim = cosine.shape[1]
    group = width // kv_local
    share = group // head_dim
    table = pl.BlockSpec((tile, head_dim), lambda i, m: (i, 0))
    in_specs = [
        pl.BlockSpec((tile, group), lambda i, m: (i, head)),
        pl.BlockSpec((tile, group), lambda i, m: (i, 0)),
        table,
        table,
        pl.BlockSpec((1, SINK_PAD, 2 * head_dim), lambda i, m: (head, 0, 0)),
        pl.BlockSpec((8, SINK_PAD), lambda i, m: (0, 0)),
    ] + [pl.BlockSpec((1, slab, 2 * head_dim), lambda i, m: (slot, 0, 0)) for _ in slabs]
    args = [meta, own, other, cosine, sine, sink, sink_pos, *slabs]
    aliases = {}
    if earlier is not None:
        in_specs.append(pl.BlockSpec(memory_space=pl.ANY))
        aliases = {len(args): 0}
        args.append(earlier)
    rows = share * tile
    work = (slab // tile) * rows * (span * slab + tile)
    return pl.pallas_call(
        functools.partial(
            attend_body, share=share, tile=tile, slab=slab, span=span, picks=picks,
            n_slabs=len(slabs),
        ),
        grid_spec=pltpu.PrefetchScalarGridSpec(
            num_scalar_prefetch=1,
            grid=(slab // tile,),
            in_specs=in_specs,
            out_specs=pl.BlockSpec((1, tile, group), lambda i, m: (request, i, head)),
            scratch_shapes=[
                pltpu.VMEM(((span + 1) * slab, head_dim), jnp.bfloat16),
                pltpu.VMEM(((span + 1) * slab, 2 * head_dim), jnp.bfloat16),
                pltpu.VMEM((rows, head_dim), jnp.bfloat16),
            ],
        ),
        out_shape=jax.ShapeDtypeStruct((num_reqs, slab, width), jnp.bfloat16),
        input_output_aliases=aliases,
        compiler_params=pltpu.CompilerParams(vmem_limit_bytes=48 << 20),
        cost_estimate=pl.CostEstimate(
            flops=8 * work * head_dim, bytes_accessed=8 << 20, transcendentals=work
        ),
        name="attend",
    )(*args)


def per_device(prompt_states, q_weight, kv_weight, lengths, sink_positions):
    num_reqs, slab, half = prompt_states.shape
    _, heads, hd = q_weight.shape
    kv_local = kv_weight.shape[2]
    count = lax.axis_size(LINE)
    n_grp = lax.axis_size("grp")
    n_seq = lax.axis_size("seq")
    grp, seq, tp = lax.axis_index("grp"), lax.axis_index("seq"), lax.axis_index("tp")
    index = grp * n_seq + seq
    span = (WINDOW - 1) // slab + 1
    tile = min(256, slab)
    assert n_grp == 2 and n_seq % 2 == 0 and span % 2 == 0 and lax.axis_size("tp") == 2

    def swap(x, axis):
        return lax.ppermute(x, axis, [(0, 1), (1, 0)])

    def forward(x, distance):
        return lax.ppermute(x, LINE, [(i - distance, i) for i in range(distance, count)])

    def pairs(x):
        return lax.ppermute(x, LINE, [(i, i ^ 1) for i in range(count)])

    def even_to_odd(x):
        return lax.ppermute(x, LINE, [(i, i + 1) for i in range(0, count, 2)])

    def odd_to_even(x):
        return lax.ppermute(x, LINE, [(i + 1, i) for i in range(0, count, 2)])

    def after(x, *first):
        return lax.optimization_barrier((x, *first))[0]

    def ordered(mine, theirs, place):
        return jnp.where(
            place == 0,
            jnp.concatenate([mine, theirs], axis=0),
            jnp.concatenate([theirs, mine], axis=0),
        )

    own_row, far_row = tp * half, (1 - tp) * half
    kv_piece = half // 2
    kv_sent = lax.dynamic_slice_in_dim(kv_weight, far_row + grp * kv_piece, kv_piece, 0)
    kv_got = swap(kv_sent, "tp")
    q_piece = half // 4
    side = lax.rem(seq, 2)
    q_sent = lax.dynamic_slice_in_dim(
        q_weight, far_row + (grp * 2 + side) * q_piece, q_piece, 0
    )
    q_got = swap(q_sent, "tp")

    def kv_matrix(w):
        return jnp.transpose(w, (0, 2, 1, 3)).reshape(w.shape[0], 2 * kv_local * hd)

    def q_matrix(w):
        return w.reshape(w.shape[0], heads * hd)

    def product(x, w):
        return jnp.dot(x, w, preferred_element_type=jnp.float32)

    kv_near = kv_matrix(lax.dynamic_slice_in_dim(kv_weight, own_row, half, 0))
    q_near = q_matrix(lax.dynamic_slice_in_dim(q_weight, own_row, half, 0))
    kv_own = [product(prompt_states[r], kv_near) for r in range(num_reqs)]

    positions = index * slab + jnp.arange(slab, dtype=jnp.int32)
    cosine, sine = rope_tables(positions, hd)
    mark_count = sink_positions.shape[1]
    marks = jnp.arange(mark_count)
    repeated = jnp.any(
        (sink_positions[:, :, None] == sink_positions[:, None, :])
        & (marks[None, :] < marks[:, None])[None],
        axis=2,
    )
    usable = jnp.where(repeated, FAR_AWAY, sink_positions)
    hits = (sink_positions[:, :, None] == positions[None, None, :]).astype(jnp.bfloat16)
    hits = jnp.pad(hits, ((0, 0), (0, 8 - mark_count), (0, 0)))
    sink_states = jnp.stack([
        product(hits[r], prompt_states[r]).astype(jnp.bfloat16) for r in range(num_reqs)
    ]).reshape(num_reqs * 8, half)
    distance = 1
    while distance < count:
        sink_states = sink_states + forward(sink_states, distance)
        distance *= 2
    sink_states = jnp.pad(sink_states, ((0, SINK_PAD - num_reqs * 8), (0, 0)))
    sink_slots = jnp.pad(sink_positions, ((0, 0), (0, 8 - mark_count))).reshape(-1)
    sink_slots = jnp.pad(sink_slots, (0, SINK_PAD - num_reqs * 8))
    sink_cos, sink_sin = rope_tables(sink_slots, hd)
    sink_lines = [
        jnp.broadcast_to(
            jnp.pad(
                usable[r], (r * 8, SINK_PAD - r * 8 - mark_count), constant_values=FAR_AWAY
            )[None, :],
            (8, SINK_PAD),
        )
        for r in range(num_reqs)
    ]

    kv_far = kv_matrix(ordered(kv_got, swap(kv_got, "grp"), grp))
    kv_part = [product(prompt_states[r], kv_far).astype(jnp.bfloat16) for r in range(num_reqs)]
    kv_other = [swap(kv_part[r], "tp") for r in range(num_reqs)]
    sink_own = product(sink_states, kv_near)
    sink_other = swap(product(sink_states, kv_far).astype(jnp.bfloat16), "tp")
    states_later = after(prompt_states, *kv_part)
    q_own = []
    for r in range(num_reqs):
        q_own.append(product(states_later[r], q_near))
    q_got = after(q_got, q_own[0])
    q_pair = ordered(q_got, pairs(q_got), side)
    q_far = q_matrix(ordered(q_pair, swap(q_pair, "grp"), grp))
    group = heads // kv_local * hd
    states_last = [after(states_later[r], q_own[r]) for r in range(num_reqs)]
    q_part = [
        [
            product(states_last[r], q_far[:, h * group:(h + 1) * group]).astype(jnp.bfloat16)
            for h in range(kv_local)
        ]
        for r in range(num_reqs)
    ]
    q_other = [[swap(q_part[r][h], "tp") for h in range(kv_local)] for r in range(num_reqs)]
    kv_other = [kv_other[0]] + [after(x, *q_part[0]) for x in kv_other[1:]]
    sink_other = after(sink_other, *q_part[0])
    sinks = finish_kv(sink_own, sink_other, sink_cos, sink_sin, 0, kv_local)

    steps = span // 2
    picks = [None] * (span + 1)

    def exchange(own):
        slabs = [own]
        relayed = [0]
        for _ in range(steps):
            slabs.append(forward(slabs[relayed[-1]], 2))
            relayed.append(len(slabs) - 1)
        slabs.append(even_to_odd(own))
        swapped = [len(slabs) - 1]
        for k in range(1, steps):
            slabs.append(pairs(slabs[relayed[k]]))
            swapped.append(len(slabs) - 1)
        slabs.append(odd_to_even(slabs[relayed[steps]]))
        last_even = len(slabs) - 1
        for k in range(steps + 1):
            picks[span - 2 * k] = (relayed[k], relayed[k])
        for k in range(1, steps + 1):
            even_pick = swapped[k] if k < steps else last_even
            picks[span - (2 * k - 1)] = (even_pick, swapped[k - 1])
        return slabs

    attended = None
    kv = []
    for r in range(num_reqs):
        meta = jnp.stack([index, lengths[r]])
        units = [(h, 1) for h in range(kv_local)] if r == 0 else [(0, kv_local)]
        mine = []
        for first, size in units:
            rows = finish_kv(kv_own[r], kv_other[r], cosine, sine, first, size)
            mine.append(rows)
            slabs = exchange(rows)
            for h in range(size):
                attended = attend(
                    meta, q_own[r], q_other[r][first + h], cosine, sine, sinks,
                    sink_lines[r], slabs, picks, span, attended, r, first + h, h,
                    num_reqs, kv_local, tile,
                )
        kv.append([m[h] for m in mine for h in range(m.shape[0])])

    lower = grp == 0
    home = jnp.stack([jnp.where(lower, kv[r][0], kv[r][1]) for r in range(num_reqs)])
    away = jnp.stack([jnp.where(lower, kv[r][1], kv[r][0]) for r in range(num_reqs)])
    came = swap(away, "grp")
    pages = jnp.stack([jnp.where(lower, home, came), jnp.where(lower, came, home)], axis=1)
    page_pos = (jnp.arange(n_grp) * n_seq + seq)[:, None] * slab + jnp.arange(slab)[None, :]
    live = page_pos[None] < lengths[:, None, None]
    pages = jnp.where(live[..., None], pages, jnp.zeros_like(pages))
    kv_cache = pages[:, None, :, None]
    return attended, kv_cache


def solution(mesh):
    placed = (
        P(None, ("grp", "seq"), "tp"),
        P(None, "tp", None),
        P(None, None, "tp", None),
        P(),
        P(),
    )

    return jax.shard_map(
        per_device,
        mesh=mesh,
        in_specs=placed,
        out_specs=(P(None, ("grp", "seq"), "tp"), P(None, ("tp", "grp"), None, "seq", None, None)),
        check_vma=False,
    )
```

```python
import functools
import math

import jax
import jax.numpy as jnp
from jax import lax
from jax.experimental import pallas as pl
from jax.experimental.pallas import tpu as pltpu
from jax.sharding import PartitionSpec as P


WINDOW = 4096
ROPE_BASE = 10000.0
NEG_FILL = -1e30
FAR_AWAY = 1 << 30
SINK_PAD = 128
LINE = ("grp", "seq")


def rope_tables(positions, head_dim):
    half_dim = head_dim // 2
    ladder = jnp.arange(half_dim, dtype=jnp.float32) * (2.0 / head_dim)
    inv_freq = jnp.exp(-math.log(ROPE_BASE) * ladder)
    angles = positions.astype(jnp.float32)[:, None] * inv_freq[None, :]
    cosine = jnp.cos(angles)
    sine = jnp.sin(angles)
    return (
        jnp.concatenate([cosine, cosine], axis=1),
        jnp.concatenate([-sine, sine], axis=1),
    )


def turn(v, cosine, sine):
    return v * cosine + pltpu.roll(v, v.shape[-1] // 2, 1) * sine


def finish_kv_body(own_ref, other_ref, cos_ref, sin_ref, out_ref):
    head_dim = cos_ref.shape[1]
    total = own_ref[...] + other_ref[...].astype(jnp.float32)
    keys = turn(total[:, :head_dim], cos_ref[...], sin_ref[...])
    out_ref[0, :, :head_dim] = keys.astype(jnp.bfloat16)
    out_ref[0, :, head_dim:] = total[:, head_dim:].astype(jnp.bfloat16)


def finish_kv(own, other, cosine, sine, first, kv_local):
    slab, _ = own.shape
    head_dim = cosine.shape[1]
    rows = min(512, slab)
    part = pl.BlockSpec((rows, 2 * head_dim), lambda g, i: (i, first + g))
    table = pl.BlockSpec((rows, head_dim), lambda g, i: (i, 0))
    return pl.pallas_call(
        finish_kv_body,
        grid=(kv_local, slab // rows),
        in_specs=[part, part, table, table],
        out_specs=pl.BlockSpec((1, rows, 2 * head_dim), lambda g, i: (g, i, 0)),
        out_shape=jax.ShapeDtypeStruct((kv_local, slab, 2 * head_dim), jnp.bfloat16),
        cost_estimate=pl.CostEstimate(
            flops=12 * kv_local * slab * head_dim, bytes_accessed=20 * kv_local * slab * head_dim, transcendentals=0
        ),
        name="finish_kv",
    )(own, other, cosine, sine)


def attend_body(meta, own_ref, other_ref, cos_ref, sin_ref, sink_ref, sink_pos_ref, *rest,
                share, tile, slab, span, picks, n_slabs):
    slab_refs = rest[:n_slabs]
    out_ref, key_buf, val_buf, q_buf = rest[-4:]
    hd = cos_ref.shape[1]
    index, length = meta[0], meta[1]
    rows = share * tile
    window = span * slab
    scale = math.log2(math.e) / math.sqrt(hd)
    block = pl.program_id(1)
    odd = lax.rem(index, 2)

    @pl.when(block == 0)
    def _():
        def place(slot, ref):
            key_buf[slot * slab:(slot + 1) * slab, :] = ref[0, :, :hd]
            val_buf[slot * slab:(slot + 1) * slab, :hd] = ref[0, :, hd:]

        for slot, (even_pick, odd_pick) in enumerate(picks):
            if even_pick == odd_pick:
                place(slot, slab_refs[even_pick])
            else:
                pl.when(odd == 0)(functools.partial(place, slot, slab_refs[even_pick]))
                pl.when(odd == 1)(functools.partial(place, slot, slab_refs[odd_pick]))
        val_buf[:, hd:] = jnp.ones((val_buf.shape[0], hd), jnp.bfloat16)

        for slot in range(span):
            @pl.when(slot < span - index)
            def _():
                start = pl.multiple_of((span - index) * slab, slab)
                key = key_buf[pl.ds(start, 16), :][:1]
                key_buf[slot * slab:(slot + 1) * slab, :] = jnp.broadcast_to(key, (slab, hd))
                val_buf[slot * slab:(slot + 1) * slab, :] = jnp.zeros((slab, 2 * hd), jnp.bfloat16)

    parts = []
    for h in range(share):
        cols = slice(h * hd, (h + 1) * hd)
        raw = own_ref[:, cols] + other_ref[:, cols].astype(jnp.float32)
        parts.append(turn(raw, cos_ref[...], sin_ref[...]).astype(jnp.bfloat16))
    q_buf[...] = jnp.concatenate(parts, axis=0)
    base = pl.multiple_of(block * tile, tile)

    def scores(start):
        keys = key_buf[pl.ds(pl.multiple_of(start, tile), tile), :]
        return lax.dot_general(
            q_buf[...], keys, (((1,), (1,)), ((), ())), preferred_element_type=jnp.float32
        )

    def vals(start):
        return val_buf[pl.ds(pl.multiple_of(start, tile), tile), :]

    def mix(p, v):
        return jnp.dot(p.astype(jnp.bfloat16), v, preferred_element_type=jnp.float32)

    q_row = lax.broadcasted_iota(jnp.int32, (share, tile, tile), 1).reshape(rows, tile)
    k_col = lax.broadcasted_iota(jnp.int32, (rows, tile), 1)
    s_own = jnp.where(k_col <= q_row, scores(base + window), NEG_FILL)
    s_far = jnp.where(k_col > q_row, scores(base), NEG_FILL)
    s_sink = lax.dot_general(
        q_buf[...], sink_ref[0, :, :hd], (((1,), (1,)), ((), ())),
        preferred_element_type=jnp.float32,
    )
    q_pos = index * slab + base + lax.broadcasted_iota(
        jnp.int32, (share, tile, SINK_PAD), 1
    ).reshape(rows, SINK_PAD)
    s_sink = jnp.where(q_pos - sink_pos_ref[0:1, :] >= WINDOW, s_sink, NEG_FILL)
    v_sink = jnp.concatenate(
        [sink_ref[0, :, hd:], jnp.ones((SINK_PAD, hd), jnp.bfloat16)], axis=1
    )

    def fold(top, acc, s, v):
        new_top = jnp.maximum(top, jnp.max(s, axis=1, keepdims=True))
        p = jnp.exp2(s * scale - new_top * scale)
        return new_top, acc * jnp.exp2((top - new_top) * scale) + mix(p, v)

    s = jnp.concatenate([s_own, s_far], axis=1)
    v = jnp.concatenate([vals(base + window), vals(base)], axis=0)
    top = jnp.max(s, axis=1, keepdims=True)
    acc = mix(jnp.exp2(s * scale - top * scale), v)
    for n in range(1, window // tile):
        start = base + n * tile
        top, acc = fold(top, acc, scores(start), vals(start))
    top, acc = fold(top, acc, s_sink, v_sink)

    pos = index * slab + base + lax.broadcasted_iota(jnp.int32, (tile, hd), 0)
    live = pos < length
    for h in range(share):
        piece = acc[h * tile:(h + 1) * tile]
        mixed = piece[:, :hd] / piece[:, hd:]
        out_ref[0, :, h * hd:(h + 1) * hd] = jnp.where(live, mixed, 0.0).astype(out_ref.dtype)


def attend(meta, own, other, cosine, sine, sink, sink_pos, slabs, picks, span, earlier,
           request, head, slot, size, num_reqs, kv_local, tile):
    slab, width = own.shape
    head_dim = cosine.shape[1]
    group = width // kv_local
    share = group // head_dim
    table = pl.BlockSpec((tile, head_dim), lambda h, i, m: (i, 0))
    in_specs = [
        pl.BlockSpec((tile, group), lambda h, i, m: (i, head + h)),
        pl.BlockSpec((tile, group), lambda h, i, m: (i, h)),
        table,
        table,
        pl.BlockSpec((1, SINK_PAD, 2 * head_dim), lambda h, i, m: (head + h, 0, 0)),
        pl.BlockSpec((8, SINK_PAD), lambda h, i, m: (0, 0)),
    ] + [pl.BlockSpec((1, slab, 2 * head_dim), lambda h, i, m: (slot + h, 0, 0)) for _ in slabs]
    args = [meta, own, other, cosine, sine, sink, sink_pos, *slabs]
    aliases = {}
    if earlier is not None:
        in_specs.append(pl.BlockSpec(memory_space=pl.ANY))
        aliases = {len(args): 0}
        args.append(earlier)
    rows = share * tile
    work = size * (slab // tile) * rows * (span * slab + tile)
    return pl.pallas_call(
        functools.partial(
            attend_body, share=share, tile=tile, slab=slab, span=span, picks=picks,
            n_slabs=len(slabs),
        ),
        grid_spec=pltpu.PrefetchScalarGridSpec(
            num_scalar_prefetch=1,
            grid=(size, slab // tile),
            in_specs=in_specs,
            out_specs=pl.BlockSpec((1, tile, group), lambda h, i, m: (request, i, head + h)),
            scratch_shapes=[
                pltpu.VMEM(((span + 1) * slab, head_dim), jnp.bfloat16),
                pltpu.VMEM(((span + 1) * slab, 2 * head_dim), jnp.bfloat16),
                pltpu.VMEM((rows, head_dim), jnp.bfloat16),
            ],
        ),
        out_shape=jax.ShapeDtypeStruct((num_reqs, slab, width), jnp.bfloat16),
        input_output_aliases=aliases,
        compiler_params=pltpu.CompilerParams(vmem_limit_bytes=48 << 20),
        cost_estimate=pl.CostEstimate(
            flops=8 * work * head_dim, bytes_accessed=size * (8 << 20), transcendentals=work
        ),
        name="attend",
    )(*args)


def per_device(prompt_states, q_weight, kv_weight, lengths, sink_positions):
    num_reqs, slab, half = prompt_states.shape
    _, heads, hd = q_weight.shape
    kv_local = kv_weight.shape[2]
    count = lax.axis_size(LINE)
    n_grp = lax.axis_size("grp")
    n_seq = lax.axis_size("seq")
    grp, seq, tp = lax.axis_index("grp"), lax.axis_index("seq"), lax.axis_index("tp")
    index = grp * n_seq + seq
    span = (WINDOW - 1) // slab + 1
    tile = min(256, slab)
    assert n_grp == 2 and n_seq % 2 == 0 and span % 2 == 0 and lax.axis_size("tp") == 2

    def swap(x, axis):
        return lax.ppermute(x, axis, [(0, 1), (1, 0)])

    def forward(x, distance):
        return lax.ppermute(x, LINE, [(i - distance, i) for i in range(distance, count)])

    def pairs(x):
        return lax.ppermute(x, LINE, [(i, i ^ 1) for i in range(count)])

    def even_to_odd(x):
        return lax.ppermute(x, LINE, [(i, i + 1) for i in range(0, count, 2)])

    def odd_to_even(x):
        return lax.ppermute(x, LINE, [(i + 1, i) for i in range(0, count, 2)])

    def after(x, *first):
        return lax.optimization_barrier((x, *first))[0]

    def ordered(mine, theirs, place):
        return jnp.where(
            place == 0,
            jnp.concatenate([mine, theirs], axis=0),
            jnp.concatenate([theirs, mine], axis=0),
        )

    own_row, far_row = tp * half, (1 - tp) * half
    kv_piece = half // 2
    kv_sent = lax.dynamic_slice_in_dim(kv_weight, far_row + grp * kv_piece, kv_piece, 0)
    kv_got = swap(kv_sent, "tp")
    q_piece = half // 4
    side = lax.rem(seq, 2)
    q_sent = lax.dynamic_slice_in_dim(
        q_weight, far_row + (grp * 2 + side) * q_piece, q_piece, 0
    )
    q_got = swap(q_sent, "tp")

    def kv_matrix(w):
        return jnp.transpose(w, (0, 2, 1, 3)).reshape(w.shape[0], 2 * kv_local * hd)

    def q_matrix(w):
        return w.reshape(w.shape[0], heads * hd)

    def product(x, w):
        return jnp.dot(x, w, preferred_element_type=jnp.float32)

    kv_near = kv_matrix(lax.dynamic_slice_in_dim(kv_weight, own_row, half, 0))
    q_near = q_matrix(lax.dynamic_slice_in_dim(q_weight, own_row, half, 0))
    kv_own = [product(prompt_states[r], kv_near) for r in range(num_reqs)]

    kv_far = kv_matrix(ordered(kv_got, swap(kv_got, "grp"), grp))
    kv_part = [product(prompt_states[r], kv_far).astype(jnp.bfloat16) for r in range(num_reqs)]
    kv_other = [swap(kv_part[r], "tp") for r in range(num_reqs)]
    states_sink = after(prompt_states, *kv_part)

    positions = index * slab + jnp.arange(slab, dtype=jnp.int32)
    cosine, sine = rope_tables(positions, hd)
    mark_count = sink_positions.shape[1]
    marks = jnp.arange(mark_count)
    repeated = jnp.any(
        (sink_positions[:, :, None] == sink_positions[:, None, :])
        & (marks[None, :] < marks[:, None])[None],
        axis=2,
    )
    usable = jnp.where(repeated, FAR_AWAY, sink_positions)
    hits = (sink_positions[:, :, None] == positions[None, None, :]).astype(jnp.bfloat16)
    hits = jnp.pad(hits, ((0, 0), (0, 8 - mark_count), (0, 0)))
    sink_states = jnp.stack([
        product(hits[r], states_sink[r]).astype(jnp.bfloat16) for r in range(num_reqs)
    ]).reshape(num_reqs * 8, half)
    distance = 1
    while distance < count:
        sink_states = sink_states + forward(sink_states, distance)
        distance *= 2
    sink_states = jnp.pad(sink_states, ((0, SINK_PAD - num_reqs * 8), (0, 0)))
    sink_slots = jnp.pad(sink_positions, ((0, 0), (0, 8 - mark_count))).reshape(-1)
    sink_slots = jnp.pad(sink_slots, (0, SINK_PAD - num_reqs * 8))
    sink_cos, sink_sin = rope_tables(sink_slots, hd)
    sink_lines = [
        jnp.broadcast_to(
            jnp.pad(
                usable[r], (r * 8, SINK_PAD - r * 8 - mark_count), constant_values=FAR_AWAY
            )[None, :],
            (8, SINK_PAD),
        )
        for r in range(num_reqs)
    ]

    sink_own = product(sink_states, kv_near)
    sink_other = swap(product(sink_states, kv_far).astype(jnp.bfloat16), "tp")
    group = heads // kv_local * hd

    def own_queries(states):
        return product(states, q_near)

    states_later = after(prompt_states, *kv_part)
    q_own = [own_queries(states_later[0])]
    q_got = after(q_got, q_own[0])
    q_pair = ordered(q_got, pairs(q_got), side)
    q_far = q_matrix(ordered(q_pair, swap(q_pair, "grp"), grp))
    q_part = [
        product(states_later[0], q_far[:, h * group:(h + 1) * group]).astype(jnp.bfloat16)
        for h in range(kv_local)
    ]
    q_first = [swap(q_part[h], "tp") for h in range(kv_local)]
    q_rest = []
    for r in range(1, num_reqs):
        q_own.append(own_queries(after(states_later[r], *q_part)))
        q_rest.append(swap(product(states_later[r], q_far).astype(jnp.bfloat16), "tp"))
    kv_other = [kv_other[0]] + [after(x, *q_part) for x in kv_other[1:]]
    sink_other = after(sink_other, *q_part)
    sinks = finish_kv(sink_own, sink_other, sink_cos, sink_sin, 0, kv_local)

    steps = span // 2
    picks = [None] * (span + 1)

    def exchange(own):
        slabs = [own]
        relayed = [0]
        for _ in range(steps):
            slabs.append(forward(slabs[relayed[-1]], 2))
            relayed.append(len(slabs) - 1)
        slabs.append(even_to_odd(own))
        swapped = [len(slabs) - 1]
        for k in range(1, steps):
            slabs.append(pairs(slabs[relayed[k]]))
            swapped.append(len(slabs) - 1)
        slabs.append(odd_to_even(slabs[relayed[steps]]))
        last_even = len(slabs) - 1
        for k in range(steps + 1):
            picks[span - 2 * k] = (relayed[k], relayed[k])
        for k in range(1, steps + 1):
            even_pick = swapped[k] if k < steps else last_even
            picks[span - (2 * k - 1)] = (even_pick, swapped[k - 1])
        return slabs

    attended = None
    kv = []
    for r in range(num_reqs):
        meta = jnp.stack([index, lengths[r]])
        kv.append(finish_kv(kv_own[r], kv_other[r], cosine, sine, 0, kv_local))
        slabs = exchange(kv[r])
        calls = [(h, 1, q_first[h]) for h in range(kv_local)]
        if r > 0:
            calls = [(0, kv_local, q_rest[r - 1])]
        for h, size, other in calls:
            attended = attend(
                meta, q_own[r], other, cosine, sine, sinks, sink_lines[r], slabs, picks,
                span, attended, r, h, h, size, num_reqs, kv_local, tile,
            )

    lower = grp == 0
    home = jnp.stack([jnp.where(lower, kv[r][0], kv[r][1]) for r in range(num_reqs)])
    away = jnp.stack([jnp.where(lower, kv[r][1], kv[r][0]) for r in range(num_reqs)])
    came = swap(away, "grp")
    pages = jnp.stack([jnp.where(lower, home, came), jnp.where(lower, came, home)], axis=1)
    page_pos = (jnp.arange(n_grp) * n_seq + seq)[:, None] * slab + jnp.arange(slab)[None, :]
    live = page_pos[None] < lengths[:, None, None]
    pages = jnp.where(live[..., None], pages, jnp.zeros_like(pages))
    kv_cache = pages[:, None, :, None]
    return attended, kv_cache


def solution(mesh):
    placed = (
        P(None, ("grp", "seq"), "tp"),
        P(None, "tp", None),
        P(None, None, "tp", None),
        P(),
        P(),
    )

    return jax.shard_map(
        per_device,
        mesh=mesh,
        in_specs=placed,
        out_specs=(P(None, ("grp", "seq"), "tp"), P(None, ("tp", "grp"), None, "seq", None, None)),
        check_vma=False,
    )
```

```python
import functools
import math

import jax
import jax.numpy as jnp
from jax import lax
from jax.experimental import pallas as pl
from jax.experimental.pallas import tpu as pltpu
from jax.sharding import PartitionSpec as P


WINDOW = 4096
ROPE_BASE = 10000.0
NEG_FILL = -1e30
FAR_AWAY = 1 << 30
SINK_PAD = 128
LINE = ("grp", "seq")


def rope_tables(positions, head_dim):
    half_dim = head_dim // 2
    ladder = jnp.arange(half_dim, dtype=jnp.float32) * (2.0 / head_dim)
    inv_freq = jnp.exp(-math.log(ROPE_BASE) * ladder)
    angles = positions.astype(jnp.float32)[:, None] * inv_freq[None, :]
    cosine = jnp.cos(angles)
    sine = jnp.sin(angles)
    return (
        jnp.concatenate([cosine, cosine], axis=1),
        jnp.concatenate([-sine, sine], axis=1),
    )


def turn(v, cosine, sine):
    return v * cosine + pltpu.roll(v, v.shape[-1] // 2, 1) * sine


def finish_kv_body(own_ref, other_ref, cos_ref, sin_ref, out_ref):
    head_dim = cos_ref.shape[1]
    total = own_ref[...] + other_ref[...].astype(jnp.float32)
    keys = turn(total[:, :head_dim], cos_ref[...], sin_ref[...])
    out_ref[0, :, :head_dim] = keys.astype(jnp.bfloat16)
    out_ref[0, :, head_dim:] = total[:, head_dim:].astype(jnp.bfloat16)


def finish_kv(own, other, cosine, sine, first, kv_local):
    slab, _ = own.shape
    head_dim = cosine.shape[1]
    rows = min(512, slab)
    part = pl.BlockSpec((rows, 2 * head_dim), lambda g, i: (i, first + g))
    table = pl.BlockSpec((rows, head_dim), lambda g, i: (i, 0))
    return pl.pallas_call(
        finish_kv_body,
        grid=(kv_local, slab // rows),
        in_specs=[part, part, table, table],
        out_specs=pl.BlockSpec((1, rows, 2 * head_dim), lambda g, i: (g, i, 0)),
        out_shape=jax.ShapeDtypeStruct((kv_local, slab, 2 * head_dim), jnp.bfloat16),
        cost_estimate=pl.CostEstimate(
            flops=12 * kv_local * slab * head_dim, bytes_accessed=20 * kv_local * slab * head_dim, transcendentals=0
        ),
        name="finish_kv",
    )(own, other, cosine, sine)


def attend_body(meta, own_ref, other_ref, cos_ref, sin_ref, sink_ref, sink_pos_ref, *rest,
                share, tile, slab, span, picks, n_slabs):
    slab_refs = rest[:n_slabs]
    out_ref, key_buf, val_buf, q_buf = rest[-4:]
    hd = cos_ref.shape[1]
    index, length = meta[0], meta[1]
    rows = share * tile
    window = span * slab
    scale = math.log2(math.e) / math.sqrt(hd)
    block = pl.program_id(1)
    odd = lax.rem(index, 2)

    @pl.when(block == 0)
    def _():
        def place(slot, ref):
            key_buf[slot * slab:(slot + 1) * slab, :] = ref[0, :, :hd]
            val_buf[slot * slab:(slot + 1) * slab, :hd] = ref[0, :, hd:]

        for slot, (even_pick, odd_pick) in enumerate(picks):
            if even_pick == odd_pick:
                place(slot, slab_refs[even_pick])
            else:
                pl.when(odd == 0)(functools.partial(place, slot, slab_refs[even_pick]))
                pl.when(odd == 1)(functools.partial(place, slot, slab_refs[odd_pick]))
        val_buf[:, hd:] = jnp.ones((val_buf.shape[0], hd), jnp.bfloat16)

        for slot in range(span):
            @pl.when(slot < span - index)
            def _():
                start = pl.multiple_of((span - index) * slab, slab)
                key = key_buf[pl.ds(start, 16), :][:1]
                key_buf[slot * slab:(slot + 1) * slab, :] = jnp.broadcast_to(key, (slab, hd))
                val_buf[slot * slab:(slot + 1) * slab, :] = jnp.zeros((slab, 2 * hd), jnp.bfloat16)

    parts = []
    for h in range(share):
        cols = slice(h * hd, (h + 1) * hd)
        raw = own_ref[:, cols] + other_ref[:, cols].astype(jnp.float32)
        parts.append(turn(raw, cos_ref[...], sin_ref[...]).astype(jnp.bfloat16))
    q_buf[...] = jnp.concatenate(parts, axis=0)
    base = pl.multiple_of(block * tile, tile)

    def scores(start):
        keys = key_buf[pl.ds(pl.multiple_of(start, tile), tile), :]
        return lax.dot_general(
            q_buf[...], keys, (((1,), (1,)), ((), ())), preferred_element_type=jnp.float32
        )

    def vals(start):
        return val_buf[pl.ds(pl.multiple_of(start, tile), tile), :]

    def mix(p, v):
        return jnp.dot(p.astype(jnp.bfloat16), v, preferred_element_type=jnp.float32)

    q_row = lax.broadcasted_iota(jnp.int32, (share, tile, tile), 1).reshape(rows, tile)
    k_col = lax.broadcasted_iota(jnp.int32, (rows, tile), 1)
    s_own = jnp.where(k_col <= q_row, scores(base + window), NEG_FILL)
    s_far = jnp.where(k_col > q_row, scores(base), NEG_FILL)
    s_sink = lax.dot_general(
        q_buf[...], sink_ref[0, :, :hd], (((1,), (1,)), ((), ())),
        preferred_element_type=jnp.float32,
    )
    q_pos = index * slab + base + lax.broadcasted_iota(
        jnp.int32, (share, tile, SINK_PAD), 1
    ).reshape(rows, SINK_PAD)
    s_sink = jnp.where(q_pos - sink_pos_ref[0:1, :] >= WINDOW, s_sink, NEG_FILL)
    v_sink = jnp.concatenate(
        [sink_ref[0, :, hd:], jnp.ones((SINK_PAD, hd), jnp.bfloat16)], axis=1
    )

    def fold(top, acc, s, v):
        new_top = jnp.maximum(top, jnp.max(s, axis=1, keepdims=True))
        p = jnp.exp2(s * scale - new_top * scale)
        return new_top, acc * jnp.exp2((top - new_top) * scale) + mix(p, v)

    s = jnp.concatenate([s_own, s_far], axis=1)
    v = jnp.concatenate([vals(base + window), vals(base)], axis=0)
    top = jnp.max(s, axis=1, keepdims=True)
    acc = mix(jnp.exp2(s * scale - top * scale), v)
    for n in range(1, window // tile):
        start = base + n * tile
        top, acc = fold(top, acc, scores(start), vals(start))
    top, acc = fold(top, acc, s_sink, v_sink)

    pos = index * slab + base + lax.broadcasted_iota(jnp.int32, (tile, hd), 0)
    live = pos < length
    for h in range(share):
        piece = acc[h * tile:(h + 1) * tile]
        mixed = piece[:, :hd] / piece[:, hd:]
        out_ref[0, :, h * hd:(h + 1) * hd] = jnp.where(live, mixed, 0.0).astype(out_ref.dtype)


def attend(meta, own, other, cosine, sine, sink, sink_pos, slabs, picks, span, earlier,
           request, head, slot, size, num_reqs, kv_local, tile):
    slab, width = own.shape
    head_dim = cosine.shape[1]
    group = width // kv_local
    share = group // head_dim
    table = pl.BlockSpec((tile, head_dim), lambda h, i, m: (i, 0))
    in_specs = [
        pl.BlockSpec((tile, group), lambda h, i, m: (i, head + h)),
        pl.BlockSpec((tile, group), lambda h, i, m: (i, head + h)),
        table,
        table,
        pl.BlockSpec((1, SINK_PAD, 2 * head_dim), lambda h, i, m: (head + h, 0, 0)),
        pl.BlockSpec((8, SINK_PAD), lambda h, i, m: (0, 0)),
    ] + [pl.BlockSpec((1, slab, 2 * head_dim), lambda h, i, m: (slot + h, 0, 0)) for _ in slabs]
    args = [meta, own, other, cosine, sine, sink, sink_pos, *slabs]
    aliases = {}
    if earlier is not None:
        in_specs.append(pl.BlockSpec(memory_space=pl.ANY))
        aliases = {len(args): 0}
        args.append(earlier)
    rows = share * tile
    work = size * (slab // tile) * rows * (span * slab + tile)
    return pl.pallas_call(
        functools.partial(
            attend_body, share=share, tile=tile, slab=slab, span=span, picks=picks,
            n_slabs=len(slabs),
        ),
        grid_spec=pltpu.PrefetchScalarGridSpec(
            num_scalar_prefetch=1,
            grid=(size, slab // tile),
            in_specs=in_specs,
            out_specs=pl.BlockSpec((1, tile, group), lambda h, i, m: (request, i, head + h)),
            scratch_shapes=[
                pltpu.VMEM(((span + 1) * slab, head_dim), jnp.bfloat16),
                pltpu.VMEM(((span + 1) * slab, 2 * head_dim), jnp.bfloat16),
                pltpu.VMEM((rows, head_dim), jnp.bfloat16),
            ],
        ),
        out_shape=jax.ShapeDtypeStruct((num_reqs, slab, width), jnp.bfloat16),
        input_output_aliases=aliases,
        compiler_params=pltpu.CompilerParams(vmem_limit_bytes=48 << 20),
        cost_estimate=pl.CostEstimate(
            flops=8 * work * head_dim, bytes_accessed=size * (8 << 20), transcendentals=work
        ),
        name="attend",
    )(*args)


def per_device(prompt_states, q_weight, kv_weight, lengths, sink_positions):
    num_reqs, slab, half = prompt_states.shape
    _, heads, hd = q_weight.shape
    kv_local = kv_weight.shape[2]
    count = lax.axis_size(LINE)
    n_grp = lax.axis_size("grp")
    n_seq = lax.axis_size("seq")
    grp, seq, tp = lax.axis_index("grp"), lax.axis_index("seq"), lax.axis_index("tp")
    index = grp * n_seq + seq
    span = (WINDOW - 1) // slab + 1
    tile = min(256, slab)
    assert n_grp == 2 and n_seq % 2 == 0 and span % 2 == 0 and lax.axis_size("tp") == 2

    def swap(x, axis):
        return lax.ppermute(x, axis, [(0, 1), (1, 0)])

    def forward(x, distance):
        return lax.ppermute(x, LINE, [(i - distance, i) for i in range(distance, count)])

    def pairs(x):
        return lax.ppermute(x, LINE, [(i, i ^ 1) for i in range(count)])

    def even_to_odd(x):
        return lax.ppermute(x, LINE, [(i, i + 1) for i in range(0, count, 2)])

    def odd_to_even(x):
        return lax.ppermute(x, LINE, [(i + 1, i) for i in range(0, count, 2)])

    def after(x, *first):
        return lax.optimization_barrier((x, *first))[0]

    def ordered(mine, theirs, place):
        return jnp.where(
            place == 0,
            jnp.concatenate([mine, theirs], axis=0),
            jnp.concatenate([theirs, mine], axis=0),
        )

    own_row, far_row = tp * half, (1 - tp) * half
    kv_piece = half // 2
    kv_sent = lax.dynamic_slice_in_dim(kv_weight, far_row + grp * kv_piece, kv_piece, 0)
    kv_got = swap(kv_sent, "tp")
    q_piece = half // 4
    side = lax.rem(seq, 2)
    q_sent = lax.dynamic_slice_in_dim(
        q_weight, far_row + (grp * 2 + side) * q_piece, q_piece, 0
    )
    q_got = swap(q_sent, "tp")

    def kv_matrix(w):
        return jnp.transpose(w, (0, 2, 1, 3)).reshape(w.shape[0], 2 * kv_local * hd)

    def q_matrix(w):
        return w.reshape(w.shape[0], heads * hd)

    def product(x, w):
        return jnp.dot(x, w, preferred_element_type=jnp.float32)

    kv_near = kv_matrix(lax.dynamic_slice_in_dim(kv_weight, own_row, half, 0))
    q_near = q_matrix(lax.dynamic_slice_in_dim(q_weight, own_row, half, 0))
    kv_own = [product(prompt_states[r], kv_near) for r in range(num_reqs)]

    kv_got = after(kv_got, kv_own[0])
    kv_far = kv_matrix(ordered(kv_got, swap(kv_got, "grp"), grp))
    kv_part = [product(prompt_states[r], kv_far).astype(jnp.bfloat16) for r in range(num_reqs)]
    kv_other = [swap(kv_part[r], "tp") for r in range(num_reqs)]
    states_sink = after(prompt_states, *kv_part)

    positions = index * slab + jnp.arange(slab, dtype=jnp.int32)
    cosine, sine = rope_tables(positions, hd)
    mark_count = sink_positions.shape[1]
    marks = jnp.arange(mark_count)
    repeated = jnp.any(
        (sink_positions[:, :, None] == sink_positions[:, None, :])
        & (marks[None, :] < marks[:, None])[None],
        axis=2,
    )
    usable = jnp.where(repeated, FAR_AWAY, sink_positions)
    hits = (sink_positions[:, :, None] == positions[None, None, :]).astype(jnp.bfloat16)
    hits = jnp.pad(hits, ((0, 0), (0, 8 - mark_count), (0, 0)))
    sink_states = jnp.stack([
        product(hits[r], states_sink[r]).astype(jnp.bfloat16) for r in range(num_reqs)
    ]).reshape(num_reqs * 8, half)
    distance = 1
    while distance < count:
        sink_states = sink_states + forward(sink_states, distance)
        distance *= 2
    sink_states = jnp.pad(sink_states, ((0, SINK_PAD - num_reqs * 8), (0, 0)))
    sink_slots = jnp.pad(sink_positions, ((0, 0), (0, 8 - mark_count))).reshape(-1)
    sink_slots = jnp.pad(sink_slots, (0, SINK_PAD - num_reqs * 8))
    sink_cos, sink_sin = rope_tables(sink_slots, hd)
    sink_lines = [
        jnp.broadcast_to(
            jnp.pad(
                usable[r], (r * 8, SINK_PAD - r * 8 - mark_count), constant_values=FAR_AWAY
            )[None, :],
            (8, SINK_PAD),
        )
        for r in range(num_reqs)
    ]

    sink_own = product(sink_states, kv_near)
    sink_other = swap(product(sink_states, kv_far).astype(jnp.bfloat16), "tp")

    def own_queries(states):
        return product(states, q_near)

    states_later = after(prompt_states, *kv_part)
    q_own = [own_queries(states_later[0])]
    q_got = after(q_got, q_own[0])
    q_pair = ordered(q_got, pairs(q_got), side)
    q_far = q_matrix(ordered(q_pair, swap(q_pair, "grp"), grp))
    q_part, q_other = [], []
    for r in range(num_reqs):
        states = states_later[r]
        if r > 0:
            q_own.append(own_queries(after(states, *q_part)))
        q_part.append(product(states, q_far).astype(jnp.bfloat16))
        q_other.append(swap(q_part[r], "tp"))
    kv_other = [kv_other[0]] + [after(x, q_part[0]) for x in kv_other[1:]]
    sink_other = after(sink_other, q_part[0])
    sinks = finish_kv(sink_own, sink_other, sink_cos, sink_sin, 0, kv_local)

    steps = span // 2
    picks = [None] * (span + 1)

    def exchange(own):
        slabs = [own]
        relayed = [0]
        for _ in range(steps):
            slabs.append(forward(slabs[relayed[-1]], 2))
            relayed.append(len(slabs) - 1)
        slabs.append(even_to_odd(own))
        swapped = [len(slabs) - 1]
        for k in range(1, steps):
            slabs.append(pairs(slabs[relayed[k]]))
            swapped.append(len(slabs) - 1)
        slabs.append(odd_to_even(slabs[relayed[steps]]))
        last_even = len(slabs) - 1
        for k in range(steps + 1):
            picks[span - 2 * k] = (relayed[k], relayed[k])
        for k in range(1, steps + 1):
            even_pick = swapped[k] if k < steps else last_even
            picks[span - (2 * k - 1)] = (even_pick, swapped[k - 1])
        return slabs

    attended = None
    kv = []
    for r in range(num_reqs):
        meta = jnp.stack([index, lengths[r]])
        kv.append(finish_kv(kv_own[r], kv_other[r], cosine, sine, 0, kv_local))
        slabs = exchange(kv[r])
        calls = [(h, 1) for h in range(kv_local)] if r == 0 else [(0, kv_local)]
        for h, size in calls:
            attended = attend(
                meta, q_own[r], q_other[r], cosine, sine, sinks, sink_lines[r], slabs, picks,
                span, attended, r, h, h, size, num_reqs, kv_local, tile,
            )

    lower = grp == 0
    home = jnp.stack([jnp.where(lower, kv[r][0], kv[r][1]) for r in range(num_reqs)])
    away = jnp.stack([jnp.where(lower, kv[r][1], kv[r][0]) for r in range(num_reqs)])
    came = swap(away, "grp")
    pages = jnp.stack([jnp.where(lower, home, came), jnp.where(lower, came, home)], axis=1)
    page_pos = (jnp.arange(n_grp) * n_seq + seq)[:, None] * slab + jnp.arange(slab)[None, :]
    live = page_pos[None] < lengths[:, None, None]
    pages = jnp.where(live[..., None], pages, jnp.zeros_like(pages))
    kv_cache = pages[:, None, :, None]
    return attended, kv_cache


def solution(mesh):
    placed = (
        P(None, ("grp", "seq"), "tp"),
        P(None, "tp", None),
        P(None, None, "tp", None),
        P(),
        P(),
    )

    return jax.shard_map(
        per_device,
        mesh=mesh,
        in_specs=placed,
        out_specs=(P(None, ("grp", "seq"), "tp"), P(None, ("tp", "grp"), None, "seq", None, None)),
        check_vma=False,
    )
```
